32 devices in a mesh: parts: 2 (over y), space: 16 (over z, x, core).
Axes of the slice: x: 2, y: 2, z: 4, core: 2. Of those that a mesh axis runs over, the one named last changes fastest.
Arguments:
- outer_grad: bfloat16 [32, 4, 128, 1024], P(('parts', 'space')), parts along dimension 0, may hold values from -6 to 6
- block_input: bfloat16 [32, 4, 128, 1024], P(('parts', 'space')), parts along dimension 0, may hold values from -6 to 6
- third_input: bfloat16 [32, 4, 128, 1024], P(('parts', 'space')), parts along dimension 0, as said below
- second_input: bfloat16 [32, 8, 256, 256], P(('parts', 'space')), parts along dimension 0, as said below
- third_weight: bfloat16 [1024, 1024], replicated, may hold values from -0.1875 to 0.1875
- group_weight: bfloat16 [1024, 288], replicated, may hold values from -0.375 to 0.375
- first_weight: bfloat16 [1024, 1024], replicated, may hold values from -0.1875 to 0.1875
Outputs:
- input_grad: bfloat16 [32, 4, 128, 1024], P(('parts', 'space')), parts along dimension 0
- third_wgrad: float32 [2048, 1024], P(('parts', 'space')), parts along dimension 0
- group_wgrad: float32 [2048, 288], P(('parts', 'space')), parts along dimension 0
- first_wgrad: float32 [2048, 1024], P(('parts', 'space')), parts along dimension 0
The draws below stay inside these ranges and needn't reach their ends.
There are 2 independent parts, one for each index of `parts`. The reference program is written for one: setup_inputs(seed, part) draws one part's arguments, and reference() takes and returns one part's arrays. A program takes and returns all parts, laid end to end along the dimension named above; an argument that names none is the same for every part. Nothing has to cross between parts.
Inputs may be any that keep to these rules, and one draw needn't show every extreme that they name: `third_input`: rectified values: zero or positive, about half of them zero. `second_input`: rectified values: zero or positive, about half of them zero.
All inputs are finite; a program needn't handle non-finite values.
Results may differ from the reference program's by a relative error of at most 0.0049.
Values may be sent and summed in bfloat16 or wider, within the bound.
A program may use at most 128 MiB of HBM per device.

```python
import math
import jax
import jax.numpy as jnp

C = 1024
GROUPS = 32
BH = 4
BW = 128
GW = 32
CS = 256
GRID_ROWS = 4
HEIGHT = 32
WIDTH = 256
POSITIONS = 8192
N_SPACE = 16


def rectified(key, shape):
    base_key, factor_key = jax.random.split(key)
    base = jnp.clip(jax.random.normal(base_key, shape, jnp.float32), -6.0, 6.0)
    factor = jnp.exp(jax.random.uniform(factor_key, shape, jnp.float32, math.log(0.5), math.log(2.0)))
    return (jnp.maximum(base, 0.0) * factor).astype(jnp.bfloat16)


def draw_third_input(key, part):
    return rectified(jax.random.fold_in(key, 31), (N_SPACE, BH, BW, C))


def draw_second_input(key, part):
    return rectified(jax.random.fold_in(key, 57), (N_SPACE, 2 * BH, 2 * BW, CS))


def raised(array, stream_key, source, target, shards_of, factor):
    owner, partner = [(jnp.arange(array.shape[position]) // (array.shape[position] // shards_of)).reshape([-1 if axis == position else 1 for axis in range(array.ndim)]) for position in (source, target)]
    chosen = jax.random.permutation(stream_key, shards_of)[partner]
    strong = (owner == chosen) | (owner == (partner + shards_of // 2) % shards_of)
    return jnp.where(strong, factor * array, array)


def block_scale(stream_key, extent, shards, smallest, largest):
    factor_of = 1.0
    for axis_at, blocks in shards:
        steps = jax.random.uniform(jax.random.fold_in(jax.random.fold_in(stream_key, 6), axis_at), (blocks,), jnp.float32, smallest / len(shards), largest / len(shards))
        factor_of = factor_of * jnp.repeat(jnp.exp(steps), extent[axis_at] // blocks).reshape((-1,) + (1,) * (len(extent) - 1 - axis_at))
    return factor_of


def noise(key, shape, deviation, bound, pieces=(), dtype=jnp.bfloat16):
    drawn = jax.random.normal(key, shape, jnp.float32) * deviation
    if len(pieces) > 0:
        drawn = block_scale(key, shape, pieces, -0.22, 0.18) * drawn
    return jnp.clip(drawn, min=-bound, max=bound).astype(dtype)


def bell_draw_with(own_key, dims, deviation, most, cuts, heavy, dtype=jnp.bfloat16):
    array = deviation * jax.random.normal(own_key, dims, jnp.float32)
    if cuts:
        array = array * block_scale(own_key, dims, cuts, -0.22, 0.18)
    return jnp.clip(raised(array, jax.random.fold_in(own_key, 3), *heavy), -most, most).astype(dtype)


def setup_inputs(seed: int = 0, part: int = 0) -> dict:
    key_of = jax.random.split(jax.random.key(seed), 8)
    part_keys = jax.random.split(jax.random.fold_in(key_of[7], part), 8)
    outer_grad = noise(part_keys[0], (N_SPACE, BH, BW, C), 1.0, 6.0, ((0, 16),))
    block_input = bell_draw_with(part_keys[1], (N_SPACE, BH, BW, C), 1.0, 6.0, ((0, 16),), (0, 3, 16, 2.0))
    third_input = draw_third_input(jax.random.fold_in(jax.random.fold_in(key_of[7], part), 71), part)
    second_input = draw_second_input(jax.random.fold_in(jax.random.fold_in(key_of[7], part), 71), part)
    third_weight = noise(key_of[4], (C, C), C ** -0.5, 0.1875)
    group_weight = noise(key_of[5], (C, 9 * GW), (9 * GW) ** -0.5, 0.375)
    first_weight = noise(key_of[6], (C, C), C ** -0.5, 0.1875)
    return dict(outer_grad=outer_grad, block_input=block_input, third_input=third_input, second_input=second_input, third_weight=third_weight, group_weight=group_weight, first_weight=first_weight)


def tiles_image(tiles):
    grid_rows = 2 * GRID_ROWS
    return tiles.reshape(grid_rows, 2, BH, BW, C).transpose(0, 2, 1, 3, 4).reshape(grid_rows * BH, 2 * BW, C)

def image_tiles(image):
    grid_rows = 2 * GRID_ROWS
    return image.reshape(grid_rows, BH, 2, BW, C).transpose(0, 2, 1, 3, 4).reshape(N_SPACE, BH, BW, C)

def blocks_image(blocks):
    shaped = blocks.reshape(GRID_ROWS, 2, 2, 2 * BH, 2 * BW, CS)
    return shaped.transpose(0, 3, 4, 1, 2, 5).reshape(HEIGHT, WIDTH, C)

def reference(outer_grad, block_input, third_input, second_input, third_weight, group_weight, first_weight):
    normalizer = 1.0 / math.sqrt(POSITIONS)
    grad_rows = tiles_image(outer_grad).reshape(POSITIONS, C)
    third_rows = tiles_image(third_input).reshape(POSITIONS, C)
    input_rows = tiles_image(block_input).reshape(POSITIONS, C)
    second_map = blocks_image(second_input)
    back_third = jnp.dot(grad_rows, third_weight.T, preferred_element_type=jnp.float32)
    inner_grad = jnp.where(third_rows > 0, back_third, 0.0).astype(jnp.bfloat16)
    third_wgrad = jnp.dot(third_rows.T, grad_rows, preferred_element_type=jnp.float32) * normalizer
    padded = jnp.pad(inner_grad.reshape(HEIGHT, WIDTH, C).astype(jnp.float32), ((1, 1), (1, 1), (0, 0)))
    kernel = group_weight.astype(jnp.float32).reshape(GROUPS, GW, 9, GW)
    second_groups = second_map.astype(jnp.float32).reshape(HEIGHT, WIDTH, GROUPS, GW)
    back_second = jnp.zeros((HEIGHT, WIDTH, GROUPS, GW), jnp.float32)
    tap_terms = []
    for tap_row in range(3):
        for tap_col in range(3):
            window = padded[2 - tap_row:2 - tap_row + HEIGHT, 2 - tap_col:2 - tap_col + WIDTH].reshape(HEIGHT, WIDTH, GROUPS, GW)
            back_second = back_second + jnp.einsum('hwgo,goi->hwgi', window, kernel[:, :, 3 * tap_row + tap_col, :])
            tap_terms.append(jnp.einsum('hwgi,hwgo->goi', second_groups, window))
    group_wgrad = jnp.stack(tap_terms, 2).reshape(C, 9 * GW) * normalizer
    first_map = jnp.where(second_map > 0, back_second.reshape(HEIGHT, WIDTH, C), 0.0).astype(jnp.bfloat16)
    first_rows = first_map.reshape(POSITIONS, C)
    first_wgrad = jnp.dot(input_rows.T, first_rows, preferred_element_type=jnp.float32) * normalizer
    summed = jnp.dot(first_rows, first_weight.T, preferred_element_type=jnp.float32) + grad_rows.astype(jnp.float32)
    input_grad = image_tiles(summed.astype(jnp.bfloat16).reshape(HEIGHT, WIDTH, C))
    return (input_grad, third_wgrad, group_wgrad, first_wgrad)
```

```python
import math

import jax
import jax.numpy as jnp
from jax import lax
from jax.sharding import PartitionSpec as P


def partner(block, axis, distance):
    count = lax.axis_size(axis)
    route = []
    for low in range(count):
        high = low | 1 << distance
        if high != low and high < count:
            route += [(low, high), (high, low)]
    return lax.ppermute(block, axis, route)


def from_behind(array, axis, by):
    count = lax.axis_size(axis)
    pairs = [(i, i + by) for i in range(count) if 0 <= i + by < count]
    return lax.ppermute(array, axis, pairs)


def halve(piece, order, bits):
    position = lax.axis_index("space")
    left = list(range(bits))[::-1]
    for bit in order:
        axis = left.index(bit)
        mine = position // (1 << bit) % 2
        sent = lax.dynamic_index_in_dim(piece, 1 - mine, axis, keepdims=False)
        kept = lax.dynamic_index_in_dim(piece, mine, axis, keepdims=False)
        received = partner(sent.astype(jnp.bfloat16), "space", bit)
        piece = kept + received.astype(jnp.float32)
        left.remove(bit)
    return piece


def sum_shards(term, pieces):
    devices = lax.axis_size("space")
    bits = devices.bit_length() - 1
    rows, columns = term.shape
    view = term.reshape((2,) * bits + (rows // devices, columns))
    low_first = list(range(bits))
    high_first = [0] + list(range(2, bits)) + [1]
    width = columns // pieces
    done = [
        halve(
            view[..., at * width : (at + 1) * width],
            (low_first, high_first)[at % 2],
            bits,
        )
        for at in range(pieces)
    ]
    return done[0] if pieces == 1 else jnp.concatenate(done, -1)


def to_groups(tile, col_parity, row_parity, row_bit):
    tile_rows, tile_width, channels = tile.shape
    shard_width = channels // 4
    split = tile.reshape(tile_rows, tile_width, 2, 2, shard_width)
    kept_part = lax.dynamic_index_in_dim(split, col_parity, 3, keepdims=False)
    sent_part = lax.dynamic_index_in_dim(split, 1 - col_parity, 3, keepdims=False)
    received = partner(sent_part, "space", 0)
    joined = jnp.where(
        col_parity == 0, jnp.stack([kept_part, received], 1), jnp.stack([received, kept_part], 1)
    )
    joined = joined.reshape(tile_rows, 2 * tile_width, 2, shard_width)
    kept_rows = lax.dynamic_index_in_dim(joined, row_parity, 2, keepdims=False)
    sent_rows = lax.dynamic_index_in_dim(joined, 1 - row_parity, 2, keepdims=False)
    received_rows = partner(sent_rows, "space", row_bit)
    stacked = jnp.where(
        row_parity == 0,
        jnp.stack([kept_rows, received_rows], 0),
        jnp.stack([received_rows, kept_rows], 0),
    )
    return stacked.reshape(2 * tile_rows, 2 * tile_width, shard_width)


def to_tiles(block, col_parity, row_parity, row_bit):
    double_rows, double_cols, shard_width = block.shape
    tile_rows = double_rows // 2
    tile_width = double_cols // 2
    split = block.reshape(2, tile_rows, double_cols, shard_width)
    kept_part = lax.dynamic_index_in_dim(split, row_parity, 0, keepdims=False)
    sent_part = lax.dynamic_index_in_dim(split, 1 - row_parity, 0, keepdims=False)
    received = partner(sent_part, "space", row_bit)
    joined = jnp.where(
        row_parity == 0, jnp.stack([kept_part, received], 2), jnp.stack([received, kept_part], 2)
    )
    joined = joined.reshape(tile_rows, 2, tile_width, 2, shard_width)
    kept_cols = lax.dynamic_index_in_dim(joined, col_parity, 1, keepdims=False)
    sent_cols = lax.dynamic_index_in_dim(joined, 1 - col_parity, 1, keepdims=False)
    received_cols = partner(sent_cols, "space", 0)
    stacked = jnp.where(
        col_parity == 0,
        jnp.stack([kept_cols, received_cols], 3),
        jnp.stack([received_cols, kept_cols], 3),
    )
    return stacked.reshape(tile_rows, tile_width, 4 * shard_width)


def with_rims(block, row_step):
    top = from_behind(block[-1:], "space", row_step)
    bottom = from_behind(block[:1], "space", -row_step)
    tall = jnp.concatenate([top, block, bottom], 0)
    empty = jnp.zeros_like(tall[:, :1])
    return jnp.concatenate([empty, tall, empty], 1)


def group_backward(padded, second_block, kernel, normalizer):
    tile_rows, tile_width, channels = second_block.shape
    group_width = kernel.shape[3]
    groups = channels // group_width
    second_groups = second_block.reshape(tile_rows, tile_width, groups, group_width)
    back_second = jnp.zeros((tile_rows, tile_width, groups, group_width), jnp.float32)
    tap_terms = []
    for tap_row in range(3):
        for tap_col in range(3):
            window = padded[
                2 - tap_row : 2 - tap_row + tile_rows, 2 - tap_col : 2 - tap_col + tile_width
            ]
            window = window.reshape(tile_rows, tile_width, groups, group_width)
            back_second = back_second + jnp.einsum(
                "hwgo,goi->hwgi",
                window,
                kernel[:, :, 3 * tap_row + tap_col, :],
                preferred_element_type=jnp.float32,
            )
            tap_terms.append(
                jnp.einsum(
                    "hwgi,hwgo->goi", second_groups, window, preferred_element_type=jnp.float32
                )
            )
    local_term = jnp.stack(tap_terms, 2).reshape(channels, 9 * group_width) * normalizer
    return (back_second.reshape(tile_rows, tile_width, channels), local_term)


def per_device(
    outer_grad, block_input, third_input, second_input, third_weight, group_weight, first_weight
):
    devices = lax.axis_size("space")
    position = lax.axis_index("space")
    row_bit = 1
    col_parity = position % 2
    row_parity = position // 2 % 2
    tile_rows = outer_grad.shape[1]
    tile_width = outer_grad.shape[2]
    channels = outer_grad.shape[3]
    shard_width = channels // 4
    group_width = group_weight.shape[1] // 9
    normalizer = 1.0 / math.sqrt(tile_rows * tile_width * devices)
    grad_rows = outer_grad.reshape(tile_rows * tile_width, channels)
    third_rows = third_input.reshape(tile_rows * tile_width, channels)
    input_rows = block_input.reshape(tile_rows * tile_width, channels)
    back_third = lax.dot_general(
        grad_rows, third_weight, (((1,), (1,)), ((), ())), preferred_element_type=jnp.float32
    )
    inner_grad = jnp.where(third_rows > 0, back_third, 0.0).astype(jnp.bfloat16)
    left_cols = third_rows
    third_wgrad = sum_shards(
        lax.dot_general(
            left_cols, grad_rows, (((0,), (0,)), ((), ())), preferred_element_type=jnp.float32
        )
        * normalizer,
        2,
    )
    inner_block = to_groups(
        inner_grad.reshape(tile_rows, tile_width, channels), col_parity, row_parity, row_bit
    )
    second_block = second_input[0]
    row_step = 4
    offset = (2 * row_parity + col_parity) * shard_width
    padded = with_rims(inner_block, row_step)
    kernel = lax.dynamic_slice_in_dim(group_weight, offset, shard_width, 0)
    kernel = kernel.reshape(shard_width // group_width, group_width, 9, group_width)
    back_second, local_term = group_backward(padded, second_block, kernel, normalizer)
    full_term = lax.dynamic_update_slice_in_dim(
        jnp.zeros((channels, 9 * group_width), jnp.float32), local_term, offset, 0
    )
    group_wgrad = sum_shards(full_term, 1)
    first_block = jnp.where(second_block > 0, back_second, 0.0).astype(jnp.bfloat16)
    first_tile = to_tiles(first_block, col_parity, row_parity, row_bit)
    first_rows = first_tile.reshape(tile_rows * tile_width, channels)
    summed = lax.dot_general(
        first_rows, first_weight, (((1,), (1,)), ((), ())), preferred_element_type=jnp.float32
    )
    input_grad = (
        (summed + grad_rows.astype(jnp.float32))
        .astype(jnp.bfloat16)
        .reshape(1, tile_rows, tile_width, channels)
    )
    left_cols = input_rows
    first_wgrad = sum_shards(
        lax.dot_general(
            left_cols, first_rows, (((0,), (0,)), ((), ())), preferred_element_type=jnp.float32
        )
        * normalizer,
        2,
    )
    return (input_grad, third_wgrad, group_wgrad, first_wgrad)


def solution(mesh):
    in_specs = (
        P(("parts", "space"), None, None, None),
        P(("parts", "space"), None, None, None),
        P(("parts", "space"), None, None, None),
        P(("parts", "space"), None, None, None),
        P(),
        P(),
        P(),
    )
    out_specs = (
        P(("parts", "space"), None, None, None),
        P(("parts", "space"), None),
        P(("parts", "space"), None),
        P(("parts", "space"), None),
    )
    return jax.shard_map(
        per_device, mesh=mesh, in_specs=in_specs, out_specs=out_specs, check_vma=False
    )
```

```python
import functools
import math

import jax
import jax.numpy as jnp
from jax import lax
from jax.experimental import pallas as pl
from jax.experimental.pallas import tpu as pltpu
from jax.sharding import PartitionSpec as P


def partner(block, axis, distance):
    count = lax.axis_size(axis)
    route = []
    for low in range(count):
        high = low | 1 << distance
        if high != low and high < count:
            route += [(low, high), (high, low)]
    return lax.ppermute(block, axis, route)


def from_behind(array, axis, by):
    count = lax.axis_size(axis)
    pairs = [(i, i + by) for i in range(count) if 0 <= i + by < count]
    return lax.ppermute(array, axis, pairs)


def halve(piece, order, bits):
    position = lax.axis_index("space")
    left = list(range(bits))[::-1]
    for bit in order:
        axis = left.index(bit)
        mine = position // (1 << bit) % 2
        sent = lax.dynamic_index_in_dim(piece, 1 - mine, axis, keepdims=False)
        kept = lax.dynamic_index_in_dim(piece, mine, axis, keepdims=False)
        received = partner(sent.astype(jnp.bfloat16), "space", bit)
        piece = kept + received.astype(jnp.float32)
        left.remove(bit)
    return piece


def sum_shards(terms):
    devices = lax.axis_size("space")
    bits = devices.bit_length() - 1
    low_first = list(range(bits))
    high_first = [0] + list(range(2, bits)) + [1]
    done = []
    for at, term in enumerate(terms):
        rows, columns = term.shape
        view = term.reshape((2,) * bits + (rows // devices, columns))
        done.append(halve(view, (low_first, high_first)[at % 2], bits))
    return done[0] if len(done) == 1 else jnp.concatenate(done, -1)


def to_tiles(block, col_parity, row_parity, row_bit):
    double_rows, double_cols, shard_width = block.shape
    tile_rows = double_rows // 2
    tile_width = double_cols // 2
    split = block.reshape(2, tile_rows, double_cols, shard_width)
    kept_part = lax.dynamic_index_in_dim(split, row_parity, 0, keepdims=False)
    sent_part = lax.dynamic_index_in_dim(split, 1 - row_parity, 0, keepdims=False)
    received = partner(sent_part, "space", row_bit)
    joined = jnp.where(
        row_parity == 0, jnp.stack([kept_part, received], 2), jnp.stack([received, kept_part], 2)
    )
    joined = joined.reshape(tile_rows, 2, tile_width, 2, shard_width)
    kept_cols = lax.dynamic_index_in_dim(joined, col_parity, 1, keepdims=False)
    sent_cols = lax.dynamic_index_in_dim(joined, 1 - col_parity, 1, keepdims=False)
    received_cols = partner(sent_cols, "space", 0)
    stacked = jnp.where(
        col_parity == 0,
        jnp.stack([kept_cols, received_cols], 3),
        jnp.stack([received_cols, kept_cols], 3),
    )
    return stacked.reshape(tile_rows, tile_width, 4 * shard_width)


def group_kernel(
    tile_rows, width, group_width, normalizer,
    inner_ref, top_ref, bottom_ref, left_ref, right_ref, second_ref, weight_ref,
    first_ref, wgrad_ref, shifted, flipped,
):
    channels = inner_ref.shape[1]
    column = lax.broadcasted_iota(jnp.int32, (width, channels), 0)
    left = left_ref[...]
    right = right_ref[...]
    for y in range(tile_rows + 2):
        if y == 0:
            piece = top_ref[...]
        elif y == tile_rows + 1:
            piece = bottom_ref[...]
        else:
            piece = inner_ref[(y - 1) * width : y * width, :]
        wide = piece.astype(jnp.float32)
        before = jnp.where(column == width - 1, right[y : y + 1], pltpu.roll(wide, width - 1, 0))
        after = jnp.where(column == 0, left[y : y + 1], pltpu.roll(wide, 1, 0))
        for at, moved in enumerate((before, wide, after)):
            shifted[at, y * width : (y + 1) * width, :] = moved.astype(jnp.bfloat16)
            flipped[at, :, y * width : (y + 1) * width] = moved.T.astype(jnp.bfloat16)
    lanes = 128
    per = lanes // group_width
    own = (
        lax.broadcasted_iota(jnp.int32, (channels, channels), 0) // group_width
        == lax.broadcasted_iota(jnp.int32, (channels, channels), 1) // group_width
    )
    lane_group = lax.broadcasted_iota(jnp.int32, (channels, lanes), 1) // group_width

    def spread(array):
        step = group_width
        while step < lanes:
            array = array + pltpu.roll(array, step, 1)
            step *= 2
        return array

    second = second_ref[...]
    size = tile_rows * width
    back = jnp.zeros((size, channels), jnp.float32)
    row = None
    for tap in range(9):
        u, v = tap // 3 - 1, tap % 3 - 1
        start = (1 - u) * width
        chunk, slot = tap // per, tap % per
        if tap < 8:
            taps = weight_ref[:, chunk * lanes : (chunk + 1) * lanes].astype(jnp.float32)
            taps = jnp.where(lane_group == slot, taps, 0.0)
        else:
            taps = weight_ref[:, 8 * group_width : 9 * group_width].astype(jnp.float32)
            taps = jnp.concatenate(
                [taps, jnp.zeros((channels, lanes - group_width), jnp.float32)], 1
            )
        taps = spread(taps)
        dense = jnp.concatenate([taps] * (channels // lanes), 1)
        dense = jnp.where(own, dense, 0.0).astype(jnp.bfloat16)
        back = back + jnp.dot(
            shifted[v + 1, start : start + size, :], dense, preferred_element_type=jnp.float32
        )
        term = jnp.dot(
            flipped[v + 1, :, start : start + size], second, preferred_element_type=jnp.float32
        )
        term = jnp.where(own, term, 0.0)
        folded = term[:, :lanes]
        for at in range(1, channels // lanes):
            folded = folded + term[:, at * lanes : (at + 1) * lanes]
        folded = spread(folded) * normalizer
        row = folded if slot == 0 else jnp.where(lane_group == slot, folded, row)
        if slot == per - 1:
            wgrad_ref[:, chunk * lanes : (chunk + 1) * lanes] = row
        elif tap == 8:
            wgrad_ref[:, 8 * group_width : 9 * group_width] = row[:, :group_width]
    first_ref[...] = jnp.where(second > 0, back, 0.0).astype(jnp.bfloat16)


def group_backward(inner, top, bottom, left, right, second, weight, tile_rows, normalizer):
    size, channels = inner.shape
    width = size // tile_rows
    taps = weight.shape[1]
    block = 256
    tall = tile_rows + 2

    def by_channels(rows):
        return pl.BlockSpec((rows, block), lambda at: (0, at))

    by_rows = pl.BlockSpec((block, taps), lambda at: (at, 0))
    return pl.pallas_call(
        functools.partial(group_kernel, tile_rows, width, taps // 9, normalizer),
        grid=(channels // block,),
        in_specs=[
            by_channels(size),
            by_channels(width),
            by_channels(width),
            by_channels(tall),
            by_channels(tall),
            by_channels(size),
            by_rows,
        ],
        out_specs=[by_channels(size), by_rows],
        out_shape=[
            jax.ShapeDtypeStruct((size, channels), jnp.bfloat16),
            jax.ShapeDtypeStruct((channels, taps), jnp.float32),
        ],
        scratch_shapes=[
            pltpu.VMEM((3, tall * width, block), jnp.bfloat16),
            pltpu.VMEM((3, block, tall * width), jnp.bfloat16),
        ],
        compiler_params=pltpu.CompilerParams(vmem_limit_bytes=32 * 2**20),
        cost_estimate=pl.CostEstimate(
            flops=36 * size * block * channels, bytes_accessed=8 * size * channels, transcendentals=0
        ),
    )(inner, top, bottom, left, right, second, weight)


def per_device(
    outer_grad, block_input, third_input, second_input, third_weight, group_weight, first_weight
):
    devices = lax.axis_size("space")
    position = lax.axis_index("space")
    row_bit = 1
    col_parity = position % 2
    row_parity = position // 2 % 2
    tile_rows = outer_grad.shape[1]
    tile_width = outer_grad.shape[2]
    channels = outer_grad.shape[3]
    normalizer = 1.0 / math.sqrt(tile_rows * tile_width * devices)
    grad_rows = outer_grad.reshape(tile_rows * tile_width, channels)
    third_rows = third_input.reshape(tile_rows * tile_width, channels)
    input_rows = block_input.reshape(tile_rows * tile_width, channels)
    back_third = lax.dot_general(
        grad_rows, third_weight, (((1,), (1,)), ((), ())), preferred_element_type=jnp.float32
    )
    inner_grad = jnp.where(third_rows > 0, back_third, 0.0).astype(jnp.bfloat16)
    half = channels // 2
    inner_tile = inner_grad.reshape(tile_rows, tile_width, channels)
    top = from_behind(inner_tile[-1:], "space", 2)
    bottom = from_behind(inner_tile[:1], "space", -2)

    def edge(tile):
        return jnp.where(col_parity == 0, tile[:, -1], tile[:, 0])

    rims = partner(
        jnp.concatenate([edge(top), edge(inner_tile), edge(bottom)], 0), "space", 0
    ).astype(jnp.float32)
    left = jnp.where(col_parity == 1, rims, 0.0)
    right = jnp.where(col_parity == 0, rims, 0.0)
    second_tile = to_tiles(second_input[0], col_parity, row_parity, row_bit)
    first_rows, local_term = group_backward(
        inner_grad,
        top[0],
        bottom[0],
        left,
        right,
        second_tile.reshape(tile_rows * tile_width, channels),
        group_weight,
        tile_rows,
        normalizer,
    )

    def half_terms(rows, columns):
        return [
            lax.dot_general(
                rows,
                columns[:, at : at + half],
                (((0,), (0,)), ((), ())),
                preferred_element_type=jnp.float32,
            )
            * normalizer
            for at in (0, half)
        ]

    third_wgrad = sum_shards(half_terms(third_rows, grad_rows))
    group_wgrad = sum_shards([local_term])
    summed = lax.dot_general(
        first_rows, first_weight, (((1,), (1,)), ((), ())), preferred_element_type=jnp.float32
    )
    input_grad = (
        (summed + grad_rows.astype(jnp.float32))
        .astype(jnp.bfloat16)
        .reshape(1, tile_rows, tile_width, channels)
    )
    first_wgrad = sum_shards(half_terms(input_rows, first_rows))
    return (input_grad, third_wgrad, group_wgrad, first_wgrad)


def solution(mesh):
    in_specs = (
        P(("parts", "space"), None, None, None),
        P(("parts", "space"), None, None, None),
        P(("parts", "space"), None, None, None),
        P(("parts", "space"), None, None, None),
        P(),
        P(),
        P(),
    )
    out_specs = (
        P(("parts", "space"), None, None, None),
        P(("parts", "space"), None),
        P(("parts", "space"), None),
        P(("parts", "space"), None),
    )
    return jax.shard_map(
        per_device, mesh=mesh, in_specs=in_specs, out_specs=out_specs, check_vma=False
    )
```

```python
import functools
import math

import jax
import jax.numpy as jnp
from jax import lax
from jax.experimental import pallas as pl
from jax.experimental.pallas import tpu as pltpu
from jax.sharding import PartitionSpec as P


def partner(block, axis, distance):
    count = lax.axis_size(axis)
    route = []
    for low in range(count):
        high = low | 1 << distance
        if high != low and high < count:
            route += [(low, high), (high, low)]
    return lax.ppermute(block, axis, route)


def from_behind(array, axis, by):
    count = lax.axis_size(axis)
    pairs = [(i, i + by) for i in range(count) if 0 <= i + by < count]
    return lax.ppermute(array, axis, pairs)


def halve(sent, kept, order, bits, gate=None):
    position = lax.axis_index("space")
    left = list(range(bits))[::-1]
    left.remove(order[0])
    piece = kept + partner(sent, "space", order[0]).astype(jnp.float32)
    for at, bit in enumerate(order[1:]):
        if at == 1 and gate is not None:
            piece, _ = lax.optimization_barrier((piece, gate))
        axis = left.index(bit)
        mine = position // (1 << bit) % 2
        sent = lax.dynamic_index_in_dim(piece, 1 - mine, axis, keepdims=False)
        kept = lax.dynamic_index_in_dim(piece, mine, axis, keepdims=False)
        received = partner(sent.astype(jnp.bfloat16), "space", bit)
        piece = kept + received.astype(jnp.float32)
        left.remove(bit)
    return piece


def shards_view(array, bits):
    rows, columns = array.shape
    return array.reshape((2,) * bits + (rows >> bits, columns))


def sum_shards(terms, bits, gate=None):
    low_first = list(range(bits))
    high_first = [0] + list(range(2, bits)) + [1]
    done = []
    for at, (sent, kept) in enumerate(terms):
        order = (low_first, high_first)[at % 2]
        done.append(
            halve(
                shards_view(sent, bits - 1), shards_view(kept, bits - 1), order, bits, gate
            )
        )
    return done[0] if len(done) == 1 else jnp.concatenate(done, -1)


def split_term(term, unit):
    mine = lax.axis_index("space") % 2
    view = term.reshape(-1, 2, unit, term.shape[1])
    sent = lax.dynamic_index_in_dim(view, 1 - mine, 1, keepdims=False)
    kept = lax.dynamic_index_in_dim(view, mine, 1, keepdims=False)
    columns = term.shape[1]
    return sent.astype(jnp.bfloat16).reshape(-1, columns), kept.reshape(-1, columns)


def wgrad_kernel(unit, normalizer, rows_ref, columns_ref, sent_ref, kept_ref):
    even = lax.axis_index("space") % 2 == 0
    term = lax.dot_general(
        rows_ref[...],
        columns_ref[...],
        (((0,), (0,)), ((), ())),
        preferred_element_type=jnp.float32,
    )
    term = term * normalizer
    sent, kept = [], []
    for at in range(0, term.shape[0], 2 * unit):
        low = term[at : at + unit]
        high = term[at + unit : at + 2 * unit]
        kept.append(jnp.where(even, low, high))
        sent.append(jnp.where(even, high, low))
    kept_ref[...] = jnp.concatenate(kept, 0)
    sent_ref[...] = jnp.concatenate(sent, 0).astype(jnp.bfloat16)


def wgrad_half(rows, columns, at, unit, normalizer):
    size, channels = rows.shape
    block = 256
    width = columns.shape[1] // 2
    out_spec = pl.BlockSpec((block // 2, width), lambda step: (step, 0))
    return pl.pallas_call(
        functools.partial(wgrad_kernel, unit, normalizer),
        grid=(channels // block,),
        in_specs=[
            pl.BlockSpec((size, block), lambda step: (0, step)),
            pl.BlockSpec((size, width), lambda step: (0, at)),
        ],
        out_specs=[out_spec, out_spec],
        out_shape=[
            jax.ShapeDtypeStruct((channels // 2, width), jnp.bfloat16),
            jax.ShapeDtypeStruct((channels // 2, width), jnp.float32),
        ],
        compiler_params=pltpu.CompilerParams(vmem_limit_bytes=24 * 2**20),
        cost_estimate=pl.CostEstimate(
            flops=2 * size * channels * width, bytes_accessed=6 * channels * width, transcendentals=0
        ),
    )(rows, columns)


def to_tiles(block, col_parity, row_parity, row_bit):
    double_rows, double_cols, shard_width = block.shape
    tile_rows = double_rows // 2
    tile_width = double_cols // 2
    split = block.reshape(2, tile_rows, double_cols, shard_width)
    kept_part = lax.dynamic_index_in_dim(split, row_parity, 0, keepdims=False)
    sent_part = lax.dynamic_index_in_dim(split, 1 - row_parity, 0, keepdims=False)
    received = partner(sent_part, "space", row_bit)
    kept_part, received = lax.optimization_barrier((kept_part, received))
    joined = jnp.where(
        row_parity == 0, jnp.stack([kept_part, received], 2), jnp.stack([received, kept_part], 2)
    )
    joined = joined.reshape(tile_rows, 2, tile_width, 2, shard_width)
    kept_cols = lax.dynamic_index_in_dim(joined, col_parity, 1, keepdims=False)
    sent_cols = lax.dynamic_index_in_dim(joined, 1 - col_parity, 1, keepdims=False)
    received_cols = partner(sent_cols, "space", 0)
    stacked = jnp.where(
        col_parity == 0,
        jnp.stack([kept_cols, received_cols], 3),
        jnp.stack([received_cols, kept_cols], 3),
    )
    return stacked.reshape(tile_rows, tile_width, 4 * shard_width), received


def group_kernel(
    tile_rows, width, group_width, normalizer,
    inner_ref, top_ref, bottom_ref, left_ref, right_ref, second_ref, weight_ref,
    first_ref, wgrad_ref, shifted, flipped,
):
    channels = inner_ref.shape[1]
    column = lax.broadcasted_iota(jnp.int32, (width, channels), 0)
    left = left_ref[...]
    right = right_ref[...]
    for y in range(tile_rows + 2):
        if y == 0:
            piece = top_ref[...]
        elif y == tile_rows + 1:
            piece = bottom_ref[...]
        else:
            piece = inner_ref[(y - 1) * width : y * width, :]
        wide = piece.astype(jnp.float32)
        before = jnp.where(column == width - 1, right[y : y + 1], pltpu.roll(wide, width - 1, 0))
        after = jnp.where(column == 0, left[y : y + 1], pltpu.roll(wide, 1, 0))
        for at, moved in enumerate((before, wide, after)):
            shifted[at, y * width : (y + 1) * width, :] = moved.astype(jnp.bfloat16)
            flipped[at, :, y * width : (y + 1) * width] = moved.T.astype(jnp.bfloat16)
    lanes = 128
    per = lanes // group_width
    own = (
        lax.broadcasted_iota(jnp.int32, (channels, channels), 0) // group_width
        == lax.broadcasted_iota(jnp.int32, (channels, channels), 1) // group_width
    )
    lane_group = lax.broadcasted_iota(jnp.int32, (channels, lanes), 1) // group_width

    def spread(array):
        step = group_width
        while step < lanes:
            array = array + pltpu.roll(array, step, 1)
            step *= 2
        return array

    second = second_ref[...]
    size = tile_rows * width
    back = jnp.zeros((size, channels), jnp.float32)
    row = None
    for tap in range(9):
        u, v = tap // 3 - 1, tap % 3 - 1
        start = (1 - u) * width
        chunk, slot = tap // per, tap % per
        if tap < 8:
            taps = weight_ref[:, chunk * lanes : (chunk + 1) * lanes].astype(jnp.float32)
            taps = jnp.where(lane_group == slot, taps, 0.0)
        else:
            taps = weight_ref[:, 8 * group_width : 9 * group_width].astype(jnp.float32)
            taps = jnp.concatenate(
                [taps, jnp.zeros((channels, lanes - group_width), jnp.float32)], 1
            )
        taps = spread(taps)
        dense = jnp.concatenate([taps] * (channels // lanes), 1)
        dense = jnp.where(own, dense, 0.0).astype(jnp.bfloat16)
        back = back + jnp.dot(
            shifted[v + 1, start : start + size, :], dense, preferred_element_type=jnp.float32
        )
        term = jnp.dot(
            flipped[v + 1, :, start : start + size], second, preferred_element_type=jnp.float32
        )
        term = jnp.where(own, term, 0.0)
        folded = term[:, :lanes]
        for at in range(1, channels // lanes):
            folded = folded + term[:, at * lanes : (at + 1) * lanes]
        folded = spread(folded) * normalizer
        row = folded if slot == 0 else jnp.where(lane_group == slot, folded, row)
        if slot == per - 1:
            wgrad_ref[:, chunk * lanes : (chunk + 1) * lanes] = row
        elif tap == 8:
            wgrad_ref[:, 8 * group_width : 9 * group_width] = row[:, :group_width]
    first_ref[...] = jnp.where(second > 0, back, 0.0).astype(jnp.bfloat16)


def group_backward(inner, top, bottom, left, right, second, weight, tile_rows, normalizer):
    size, channels = inner.shape
    width = size // tile_rows
    taps = weight.shape[1]
    block = 256
    tall = tile_rows + 2

    def by_channels(rows):
        return pl.BlockSpec((rows, block), lambda at: (0, at))

    by_rows = pl.BlockSpec((block, taps), lambda at: (at, 0))
    return pl.pallas_call(
        functools.partial(group_kernel, tile_rows, width, taps // 9, normalizer),
        grid=(channels // block,),
        in_specs=[
            by_channels(size),
            by_channels(width),
            by_channels(width),
            by_channels(tall),
            by_channels(tall),
            by_channels(size),
            by_rows,
        ],
        out_specs=[by_channels(size), by_rows],
        out_shape=[
            jax.ShapeDtypeStruct((size, channels), jnp.bfloat16),
            jax.ShapeDtypeStruct((channels, taps), jnp.float32),
        ],
        scratch_shapes=[
            pltpu.VMEM((3, tall * width, block), jnp.bfloat16),
            pltpu.VMEM((3, block, tall * width), jnp.bfloat16),
        ],
        compiler_params=pltpu.CompilerParams(vmem_limit_bytes=32 * 2**20),
        cost_estimate=pl.CostEstimate(
            flops=90 * size * block * channels, bytes_accessed=8 * size * channels, transcendentals=0
        ),
    )(inner, top, bottom, left, right, second, weight)


def per_device(
    outer_grad, block_input, third_input, second_input, third_weight, group_weight, first_weight
):
    devices = lax.axis_size("space")
    position = lax.axis_index("space")
    row_bit = 1
    col_parity = position % 2
    row_parity = position // 2 % 2
    tile_rows = outer_grad.shape[1]
    tile_width = outer_grad.shape[2]
    channels = outer_grad.shape[3]
    normalizer = 1.0 / math.sqrt(tile_rows * tile_width * devices)
    grad_rows = outer_grad.reshape(tile_rows * tile_width, channels)
    third_rows = third_input.reshape(tile_rows * tile_width, channels)
    input_rows = block_input.reshape(tile_rows * tile_width, channels)
    back_third = lax.dot_general(
        grad_rows, third_weight, (((1,), (1,)), ((), ())), preferred_element_type=jnp.float32
    )
    inner_grad = jnp.where(third_rows > 0, back_third, 0.0).astype(jnp.bfloat16)
    bits = devices.bit_length() - 1
    unit = channels // devices
    inner_tile = inner_grad.reshape(tile_rows, tile_width, channels)
    top = from_behind(inner_tile[-1:], "space", 2)
    bottom = from_behind(inner_tile[:1], "space", -2)

    def edge(tile):
        return jnp.where(col_parity == 0, tile[:, -1], tile[:, 0])

    rims = partner(
        jnp.concatenate([edge(top), edge(inner_tile), edge(bottom)], 0), "space", 0
    ).astype(jnp.float32)
    left = jnp.where(col_parity == 1, rims, 0.0)
    right = jnp.where(col_parity == 0, rims, 0.0)
    second_tile, arrived = to_tiles(second_input[0], col_parity, row_parity, row_bit)
    first_rows, local_term = group_backward(
        inner_grad,
        top[0],
        bottom[0],
        left,
        right,
        second_tile.reshape(tile_rows * tile_width, channels),
        group_weight,
        tile_rows,
        normalizer,
    )

    gated_rows, _ = lax.optimization_barrier((third_rows, arrived))
    third_terms = [wgrad_half(gated_rows, grad_rows, at, unit, normalizer) for at in (0, 1)]
    third_wgrad = sum_shards(third_terms, bits, first_rows)
    first_terms = [wgrad_half(input_rows, first_rows, at, unit, normalizer) for at in (0, 1)]
    first_wgrad = sum_shards(first_terms, bits)
    group_wgrad = sum_shards([split_term(local_term, unit)], bits)
    first_rows, _ = lax.optimization_barrier((first_rows, first_terms[1][0]))
    summed = lax.dot_general(
        first_rows, first_weight, (((1,), (1,)), ((), ())), preferred_element_type=jnp.float32
    )
    input_grad = (
        (summed + grad_rows.astype(jnp.float32))
        .astype(jnp.bfloat16)
        .reshape(1, tile_rows, tile_width, channels)
    )
    return (input_grad, third_wgrad, group_wgrad, first_wgrad)


def solution(mesh):
    in_specs = (
        P(("parts", "space"), None, None, None),
        P(("parts", "space"), None, None, None),
        P(("parts", "space"), None, None, None),
        P(("parts", "space"), None, None, None),
        P(),
        P(),
        P(),
    )
    out_specs = (
        P(("parts", "space"), None, None, None),
        P(("parts", "space"), None),
        P(("parts", "space"), None),
        P(("parts", "space"), None),
    )
    return jax.shard_map(
        per_device, mesh=mesh, in_specs=in_specs, out_specs=out_specs, check_vma=False
    )
```

```python
import functools
import math

import jax
import jax.numpy as jnp
from jax import lax
from jax.experimental import pallas as pl
from jax.experimental.pallas import tpu as pltpu
from jax.sharding import PartitionSpec as P


def partner(block, axis, distance):
    count = lax.axis_size(axis)
    route = []
    for low in range(count):
        high = low | 1 << distance
        if high != low and high < count:
            route += [(low, high), (high, low)]
    return lax.ppermute(block, axis, route)


def from_behind(array, axis, by):
    count = lax.axis_size(axis)
    pairs = [(i, i + by) for i in range(count) if 0 <= i + by < count]
    return lax.ppermute(array, axis, pairs)


def halve_round(piece, left, bit):
    axis = left.index(bit)
    mine = lax.axis_index("space") // (1 << bit) % 2
    sent = lax.dynamic_index_in_dim(piece, 1 - mine, axis, keepdims=False)
    kept = lax.dynamic_index_in_dim(piece, mine, axis, keepdims=False)
    received = partner(sent.astype(jnp.bfloat16), "space", bit)
    left.remove(bit)
    return kept + received.astype(jnp.float32)


def halve_start(pair, bits):
    sent, kept = pair
    received = partner(shards_view(sent, bits - 1), "space", 0)
    return shards_view(kept, bits - 1) + received.astype(jnp.float32)


def shards_view(array, bits):
    rows, columns = array.shape
    return array.reshape((2,) * bits + (rows >> bits, columns))


def split_term(term, unit):
    mine = lax.axis_index("space") % 2
    view = term.reshape(-1, 2, unit, term.shape[1])
    sent = lax.dynamic_index_in_dim(view, 1 - mine, 1, keepdims=False)
    kept = lax.dynamic_index_in_dim(view, mine, 1, keepdims=False)
    columns = term.shape[1]
    return sent.astype(jnp.bfloat16).reshape(-1, columns), kept.reshape(-1, columns)


def wgrad_kernel(unit, normalizer, rows_ref, columns_ref, sent_ref, kept_ref):
    even = lax.axis_index("space") % 2 == 0
    term = lax.dot_general(
        rows_ref[...],
        columns_ref[...],
        (((0,), (0,)), ((), ())),
        preferred_element_type=jnp.float32,
    )
    term = term * normalizer
    sent, kept = [], []
    for at in range(0, term.shape[0], 2 * unit):
        low = term[at : at + unit]
        high = term[at + unit : at + 2 * unit]
        kept.append(jnp.where(even, low, high))
        sent.append(jnp.where(even, high, low))
    kept_ref[...] = jnp.concatenate(kept, 0)
    sent_ref[...] = jnp.concatenate(sent, 0).astype(jnp.bfloat16)


def wgrad_half(rows, columns, at, unit, normalizer):
    size, channels = rows.shape
    block = 256
    width = columns.shape[1] // 2
    out_spec = pl.BlockSpec((block // 2, width), lambda step: (step, 0))
    return pl.pallas_call(
        functools.partial(wgrad_kernel, unit, normalizer),
        grid=(channels // block,),
        in_specs=[
            pl.BlockSpec((size, block), lambda step: (0, step)),
            pl.BlockSpec((size, width), lambda step: (0, at)),
        ],
        out_specs=[out_spec, out_spec],
        out_shape=[
            jax.ShapeDtypeStruct((channels // 2, width), jnp.bfloat16),
            jax.ShapeDtypeStruct((channels // 2, width), jnp.float32),
        ],
        compiler_params=pltpu.CompilerParams(vmem_limit_bytes=24 * 2**20),
        cost_estimate=pl.CostEstimate(
            flops=2 * size * channels * width, bytes_accessed=6 * channels * width, transcendentals=0
        ),
    )(rows, columns)


def to_tiles(kept_part, sent_part, col_parity, row_parity, row_bit):
    tile_rows, double_cols, shard_width = kept_part.shape
    received = partner(sent_part, "space", row_bit)
    joined = jnp.where(
        row_parity == 0, jnp.stack([kept_part, received], 0), jnp.stack([received, kept_part], 0)
    )
    joined = joined.reshape(2, tile_rows, 2, double_cols // 2, shard_width)
    kept_cols = lax.dynamic_index_in_dim(joined, col_parity, 2, keepdims=False)
    sent_cols = lax.dynamic_index_in_dim(joined, 1 - col_parity, 2, keepdims=False)
    received_cols = partner(sent_cols, "space", 0)
    stacked = jnp.where(
        col_parity == 0,
        jnp.stack([kept_cols, received_cols], 1),
        jnp.stack([received_cols, kept_cols], 1),
    )
    return stacked.reshape(4, tile_rows * double_cols // 2, shard_width)


def group_kernel(
    tile_rows, width, group_width, normalizer,
    inner_ref, top_ref, bottom_ref, left_ref, right_ref, second_ref, weight_ref,
    first_ref, wgrad_ref, shifted, flipped,
):
    channels = inner_ref.shape[1]
    column = lax.broadcasted_iota(jnp.int32, (width, channels), 0)
    left = left_ref[...]
    right = right_ref[...]
    for y in range(tile_rows + 2):
        if y == 0:
            piece = top_ref[...]
        elif y == tile_rows + 1:
            piece = bottom_ref[...]
        else:
            piece = inner_ref[(y - 1) * width : y * width, :]
        wide = piece.astype(jnp.float32)
        before = jnp.where(column == width - 1, right[y : y + 1], pltpu.roll(wide, width - 1, 0))
        after = jnp.where(column == 0, left[y : y + 1], pltpu.roll(wide, 1, 0))
        for at, moved in enumerate((before, wide, after)):
            shifted[at, y * width : (y + 1) * width, :] = moved.astype(jnp.bfloat16)
            flipped[at, :, y * width : (y + 1) * width] = moved.T.astype(jnp.bfloat16)
    lanes = 128
    per = lanes // group_width
    own = (
        lax.broadcasted_iota(jnp.int32, (channels, channels), 0) // group_width
        == lax.broadcasted_iota(jnp.int32, (channels, channels), 1) // group_width
    )
    lane_group = lax.broadcasted_iota(jnp.int32, (channels, lanes), 1) // group_width

    def spread(array):
        step = group_width
        while step < lanes:
            array = array + pltpu.roll(array, step, 1)
            step *= 2
        return array

    second = second_ref[...]
    size = tile_rows * width
    back = jnp.zeros((size, channels), jnp.float32)
    row = None
    for tap in range(9):
        u, v = tap // 3 - 1, tap % 3 - 1
        start = (1 - u) * width
        chunk, slot = tap // per, tap % per
        if tap < 8:
            taps = weight_ref[:, chunk * lanes : (chunk + 1) * lanes].astype(jnp.float32)
            taps = jnp.where(lane_group == slot, taps, 0.0)
        else:
            taps = weight_ref[:, 8 * group_width : 9 * group_width].astype(jnp.float32)
            taps = jnp.concatenate(
                [taps, jnp.zeros((channels, lanes - group_width), jnp.float32)], 1
            )
        taps = spread(taps)
        dense = jnp.concatenate([taps] * (channels // lanes), 1)
        dense = jnp.where(own, dense, 0.0).astype(jnp.bfloat16)
        back = back + jnp.dot(
            shifted[v + 1, start : start + size, :], dense, preferred_element_type=jnp.float32
        )
        term = jnp.dot(
            flipped[v + 1, :, start : start + size], second, preferred_element_type=jnp.float32
        )
        term = jnp.where(own, term, 0.0)
        folded = term[:, :lanes]
        for at in range(1, channels // lanes):
            folded = folded + term[:, at * lanes : (at + 1) * lanes]
        folded = spread(folded) * normalizer
        row = folded if slot == 0 else jnp.where(lane_group == slot, folded, row)
        if slot == per - 1:
            wgrad_ref[:, chunk * lanes : (chunk + 1) * lanes] = row
        elif tap == 8:
            wgrad_ref[:, 8 * group_width : 9 * group_width] = row[:, :group_width]
    first_ref[...] = jnp.where(second > 0, back, 0.0).astype(jnp.bfloat16)


def group_backward(inner, top, bottom, left, right, second, weight, tile_rows, normalizer):
    size, channels = inner.shape
    width = size // tile_rows
    taps = weight.shape[1]
    block = second.shape[2]
    tall = tile_rows + 2

    def by_channels(rows):
        return pl.BlockSpec((rows, block), lambda at: (0, at))

    by_rows = pl.BlockSpec((block, taps), lambda at: (at, 0))
    return pl.pallas_call(
        functools.partial(group_kernel, tile_rows, width, taps // 9, normalizer),
        grid=(channels // block,),
        in_specs=[
            by_channels(size),
            by_channels(width),
            by_channels(width),
            by_channels(tall),
            by_channels(tall),
            pl.BlockSpec((None, size, block), lambda at: (at, 0, 0)),
            by_rows,
        ],
        out_specs=[by_channels(size), by_rows],
        out_shape=[
            jax.ShapeDtypeStruct((size, channels), jnp.bfloat16),
            jax.ShapeDtypeStruct((channels, taps), jnp.float32),
        ],
        scratch_shapes=[
            pltpu.VMEM((3, tall * width, block), jnp.bfloat16),
            pltpu.VMEM((3, block, tall * width), jnp.bfloat16),
        ],
        compiler_params=pltpu.CompilerParams(vmem_limit_bytes=32 * 2**20),
        cost_estimate=pl.CostEstimate(
            flops=90 * size * block * channels, bytes_accessed=8 * size * channels, transcendentals=0
        ),
    )(inner, top, bottom, left, right, second, weight)


def per_device(
    outer_grad, block_input, third_input, second_input, third_weight, group_weight, first_weight
):
    devices = lax.axis_size("space")
    position = lax.axis_index("space")
    row_bit = 1
    col_parity = position % 2
    row_parity = position // 2 % 2
    tile_rows = outer_grad.shape[1]
    tile_width = outer_grad.shape[2]
    channels = outer_grad.shape[3]
    normalizer = 1.0 / math.sqrt(tile_rows * tile_width * devices)
    grad_rows = outer_grad.reshape(tile_rows * tile_width, channels)
    third_rows = third_input.reshape(tile_rows * tile_width, channels)
    input_rows = block_input.reshape(tile_rows * tile_width, channels)
    split = second_input[0].reshape(2, tile_rows, 2 * tile_width, second_input.shape[3])
    kept_part = lax.dynamic_index_in_dim(split, row_parity, 0, keepdims=False)
    sent_part = lax.dynamic_index_in_dim(split, 1 - row_parity, 0, keepdims=False)
    sent_part, early_rows = lax.optimization_barrier((sent_part, grad_rows))
    back_third = lax.dot_general(
        early_rows, third_weight, (((1,), (1,)), ((), ())), preferred_element_type=jnp.float32
    )
    inner_grad = jnp.where(third_rows > 0, back_third, 0.0).astype(jnp.bfloat16)
    bits = devices.bit_length() - 1
    unit = channels // devices
    inner_tile = inner_grad.reshape(tile_rows, tile_width, channels)
    top = from_behind(inner_tile[-1:], "space", 2)
    bottom = from_behind(inner_tile[:1], "space", -2)

    def edge(tile):
        return jnp.where(col_parity == 0, tile[:, -1], tile[:, 0])

    rims = partner(
        jnp.concatenate([edge(top), edge(inner_tile), edge(bottom)], 0), "space", 0
    ).astype(jnp.float32)
    left = jnp.where(col_parity == 1, rims, 0.0)
    right = jnp.where(col_parity == 0, rims, 0.0)
    second_tile = to_tiles(kept_part, sent_part, col_parity, row_parity, row_bit)
    first_rows, local_term = group_backward(
        inner_grad,
        top[0],
        bottom[0],
        left,
        right,
        second_tile,
        group_weight,
        tile_rows,
        normalizer,
    )

    high_first = list(range(2, bits)) + [1]
    low_first = list(range(1, bits))
    third = []
    third_left = []
    for at in (0, 1):
        piece = halve_start(wgrad_half(third_rows, grad_rows, at, unit, normalizer), bits)
        left = list(range(1, bits))[::-1]
        third.append(halve_round(piece, left, high_first[0]))
        third_left.append(left)
    first_terms = [wgrad_half(input_rows, first_rows, at, unit, normalizer) for at in (0, 1)]
    group_pair = split_term(local_term, unit)
    third[0], third[1], _ = lax.optimization_barrier((third[0], third[1], first_terms[0][0]))
    last = [halve_start(pair, bits) for pair in first_terms + [group_pair]]
    last_left = [list(range(1, bits))[::-1] for _ in last]
    last_order = [low_first, high_first, high_first]
    for at in range(len(high_first)):
        if at + 1 < len(high_first):
            third = [
                halve_round(piece, left, high_first[at + 1])
                for piece, left in zip(third, third_left)
            ]
        tied = lax.optimization_barrier((*third, *last))
        third, last = list(tied[:2]), list(tied[2:])
        last = [
            halve_round(piece, left, order[at])
            for piece, left, order in zip(last, last_left, last_order)
        ]
    third_wgrad = jnp.concatenate(third, -1)
    first_wgrad = jnp.concatenate(last[:2], -1)
    group_wgrad = last[2]
    first_rows, _ = lax.optimization_barrier((first_rows, first_terms[1][0]))
    summed = lax.dot_general(
        first_rows, first_weight, (((1,), (1,)), ((), ())), preferred_element_type=jnp.float32
    )
    input_grad = (
        (summed + grad_rows.astype(jnp.float32))
        .astype(jnp.bfloat16)
        .reshape(1, tile_rows, tile_width, channels)
    )
    return (input_grad, third_wgrad, group_wgrad, first_wgrad)


def solution(mesh):
    in_specs = (
        P(("parts", "space"), None, None, None),
        P(("parts", "space"), None, None, None),
        P(("parts", "space"), None, None, None),
        P(("parts", "space"), None, None, None),
        P(),
        P(),
        P(),
    )
    out_specs = (
        P(("parts", "space"), None, None, None),
        P(("parts", "space"), None),
        P(("parts", "space"), None),
        P(("parts", "space"), None),
    )
    return jax.shard_map(
        per_device, mesh=mesh, in_specs=in_specs, out_specs=out_specs, check_vma=False
    )
```

```python
import functools
import math

import jax
import jax.numpy as jnp
from jax import lax
from jax.experimental import pallas as pl
from jax.experimental.pallas import tpu as pltpu
from jax.sharding import PartitionSpec as P


def partner(block, axis, distance):
    count = lax.axis_size(axis)
    route = []
    for low in range(count):
        high = low | 1 << distance
        if high != low and high < count:
            route += [(low, high), (high, low)]
    return lax.ppermute(block, axis, route)


def from_behind(array, axis, by):
    count = lax.axis_size(axis)
    pairs = [(i, i + by) for i in range(count) if 0 <= i + by < count]
    return lax.ppermute(array, axis, pairs)


def halve_round(piece, left, bit):
    axis = left.index(bit)
    mine = lax.axis_index("space") // (1 << bit) % 2
    sent = lax.dynamic_index_in_dim(piece, 1 - mine, axis, keepdims=False)
    kept = lax.dynamic_index_in_dim(piece, mine, axis, keepdims=False)
    received = partner(sent.astype(jnp.bfloat16), "space", bit)
    left.remove(bit)
    return kept + received.astype(jnp.float32)


def halve_start(pair, bits):
    sent, kept = pair
    received = partner(shards_view(sent, bits - 1), "space", 0)
    return shards_view(kept, bits - 1) + received.astype(jnp.float32)


def shards_view(array, bits):
    rows, columns = array.shape
    return array.reshape((2,) * bits + (rows >> bits, columns))


def split_term(term, unit):
    mine = lax.axis_index("space") % 2
    view = term.reshape(-1, 2, unit, term.shape[1])
    sent = lax.dynamic_index_in_dim(view, 1 - mine, 1, keepdims=False)
    kept = lax.dynamic_index_in_dim(view, mine, 1, keepdims=False)
    columns = term.shape[1]
    return sent.astype(jnp.bfloat16).reshape(-1, columns), kept.reshape(-1, columns)


def wgrad_kernel(unit, normalizer, rows_ref, columns_ref, sent_ref, kept_ref):
    even = lax.axis_index("space") % 2 == 0
    term = lax.dot_general(
        rows_ref[...],
        columns_ref[...],
        (((0,), (0,)), ((), ())),
        preferred_element_type=jnp.float32,
    )
    term = term * normalizer
    sent, kept = [], []
    for at in range(0, term.shape[0], 2 * unit):
        low = term[at : at + unit]
        high = term[at + unit : at + 2 * unit]
        kept.append(jnp.where(even, low, high))
        sent.append(jnp.where(even, high, low))
    kept_ref[...] = jnp.concatenate(kept, 0)
    sent_ref[...] = jnp.concatenate(sent, 0).astype(jnp.bfloat16)


def wgrad_half(rows, columns, at, unit, normalizer):
    size, channels = rows.shape
    block = 256
    width = columns.shape[1] // 2
    out_spec = pl.BlockSpec((block // 2, width), lambda step: (step, 0))
    return pl.pallas_call(
        functools.partial(wgrad_kernel, unit, normalizer),
        grid=(channels // block,),
        in_specs=[
            pl.BlockSpec((size, block), lambda step: (0, step)),
            pl.BlockSpec((size, width), lambda step: (0, at)),
        ],
        out_specs=[out_spec, out_spec],
        out_shape=[
            jax.ShapeDtypeStruct((channels // 2, width), jnp.bfloat16),
            jax.ShapeDtypeStruct((channels // 2, width), jnp.float32),
        ],
        compiler_params=pltpu.CompilerParams(vmem_limit_bytes=24 * 2**20),
        cost_estimate=pl.CostEstimate(
            flops=2 * size * channels * width, bytes_accessed=6 * channels * width, transcendentals=0
        ),
    )(rows, columns)


def to_tiles(kept_part, sent_part, col_parity, row_parity, row_bit):
    tile_rows, double_cols, shard_width = kept_part.shape
    received = partner(sent_part, "space", row_bit)
    joined = jnp.where(
        row_parity == 0, jnp.stack([kept_part, received], 0), jnp.stack([received, kept_part], 0)
    )
    joined = joined.reshape(2, tile_rows, 2, double_cols // 2, shard_width)
    kept_cols = lax.dynamic_index_in_dim(joined, col_parity, 2, keepdims=False)
    sent_cols = lax.dynamic_index_in_dim(joined, 1 - col_parity, 2, keepdims=False)
    received_cols = partner(sent_cols, "space", 0)
    stacked = jnp.where(
        col_parity == 0,
        jnp.stack([kept_cols, received_cols], 1),
        jnp.stack([received_cols, kept_cols], 1),
    )
    return stacked.reshape(4, tile_rows * double_cols // 2, shard_width)


def group_kernel(
    tile_rows, width, group_width, normalizer,
    inner_ref, top_ref, bottom_ref, left_ref, right_ref, second_ref, weight_ref,
    first_ref, wgrad_ref, shifted, flipped,
):
    channels = inner_ref.shape[1]
    column = lax.broadcasted_iota(jnp.int32, (width, channels), 0)
    left = left_ref[...]
    right = right_ref[...]
    for y in range(tile_rows + 2):
        if y == 0:
            piece = top_ref[...]
        elif y == tile_rows + 1:
            piece = bottom_ref[...]
        else:
            piece = inner_ref[(y - 1) * width : y * width, :]
        wide = piece.astype(jnp.float32)
        before = jnp.where(column == width - 1, right[y : y + 1], pltpu.roll(wide, width - 1, 0))
        after = jnp.where(column == 0, left[y : y + 1], pltpu.roll(wide, 1, 0))
        for at, moved in enumerate((before, wide, after)):
            shifted[at, y * width : (y + 1) * width, :] = moved.astype(jnp.bfloat16)
            flipped[at, :, y * width : (y + 1) * width] = moved.T.astype(jnp.bfloat16)
    lanes = 128
    per = lanes // group_width
    own = (
        lax.broadcasted_iota(jnp.int32, (channels, channels), 0) // group_width
        == lax.broadcasted_iota(jnp.int32, (channels, channels), 1) // group_width
    )
    lane_group = lax.broadcasted_iota(jnp.int32, (channels, lanes), 1) // group_width

    def spread(array):
        step = group_width
        while step < lanes:
            array = array + pltpu.roll(array, step, 1)
            step *= 2
        return array

    second = second_ref[...]
    size = tile_rows * width
    back = jnp.zeros((size, channels), jnp.float32)
    row = None
    for tap in range(9):
        u, v = tap // 3 - 1, tap % 3 - 1
        start = (1 - u) * width
        chunk, slot = tap // per, tap % per
        if tap < 8:
            taps = weight_ref[:, chunk * lanes : (chunk + 1) * lanes].astype(jnp.float32)
            taps = jnp.where(lane_group == slot, taps, 0.0)
        else:
            taps = weight_ref[:, 8 * group_width : 9 * group_width].astype(jnp.float32)
            taps = jnp.concatenate(
                [taps, jnp.zeros((channels, lanes - group_width), jnp.float32)], 1
            )
        taps = spread(taps)
        dense = jnp.concatenate([taps] * (channels // lanes), 1)
        dense = jnp.where(own, dense, 0.0).astype(jnp.bfloat16)
        back = back + jnp.dot(
            shifted[v + 1, start : start + size, :], dense, preferred_element_type=jnp.float32
        )
        term = jnp.dot(
            flipped[v + 1, :, start : start + size], second, preferred_element_type=jnp.float32
        )
        term = jnp.where(own, term, 0.0)
        folded = term[:, :lanes]
        for at in range(1, channels // lanes):
            folded = folded + term[:, at * lanes : (at + 1) * lanes]
        folded = spread(folded) * normalizer
        row = folded if slot == 0 else jnp.where(lane_group == slot, folded, row)
        if slot == per - 1:
            wgrad_ref[:, chunk * lanes : (chunk + 1) * lanes] = row
        elif tap == 8:
            wgrad_ref[:, 8 * group_width : 9 * group_width] = row[:, :group_width]
    first_ref[...] = jnp.where(second > 0, back, 0.0).astype(jnp.bfloat16)


def group_backward(inner, top, bottom, left, right, second, weight, tile_rows, normalizer):
    size, channels = inner.shape
    width = size // tile_rows
    taps = weight.shape[1]
    block = second.shape[2]
    tall = tile_rows + 2

    def by_channels(rows):
        return pl.BlockSpec((rows, block), lambda at: (0, at))

    by_rows = pl.BlockSpec((block, taps), lambda at: (at, 0))
    return pl.pallas_call(
        functools.partial(group_kernel, tile_rows, width, taps // 9, normalizer),
        grid=(channels // block,),
        in_specs=[
            by_channels(size),
            by_channels(width),
            by_channels(width),
            by_channels(tall),
            by_channels(tall),
            pl.BlockSpec((None, size, block), lambda at: (at, 0, 0)),
            by_rows,
        ],
        out_specs=[by_channels(size), by_rows],
        out_shape=[
            jax.ShapeDtypeStruct((size, channels), jnp.bfloat16),
            jax.ShapeDtypeStruct((channels, taps), jnp.float32),
        ],
        scratch_shapes=[
            pltpu.VMEM((3, tall * width, block), jnp.bfloat16),
            pltpu.VMEM((3, block, tall * width), jnp.bfloat16),
        ],
        compiler_params=pltpu.CompilerParams(vmem_limit_bytes=32 * 2**20),
        cost_estimate=pl.CostEstimate(
            flops=90 * size * block * channels, bytes_accessed=8 * size * channels, transcendentals=0
        ),
    )(inner, top, bottom, left, right, second, weight)


def per_device(
    outer_grad, block_input, third_input, second_input, third_weight, group_weight, first_weight
):
    devices = lax.axis_size("space")
    position = lax.axis_index("space")
    row_bit = 1
    col_parity = position % 2
    row_parity = position // 2 % 2
    tile_rows = outer_grad.shape[1]
    tile_width = outer_grad.shape[2]
    channels = outer_grad.shape[3]
    normalizer = 1.0 / math.sqrt(tile_rows * tile_width * devices)
    grad_rows = outer_grad.reshape(tile_rows * tile_width, channels)
    third_rows = third_input.reshape(tile_rows * tile_width, channels)
    input_rows = block_input.reshape(tile_rows * tile_width, channels)
    split = second_input[0].reshape(2, tile_rows, 2 * tile_width, second_input.shape[3])
    kept_part = lax.dynamic_index_in_dim(split, row_parity, 0, keepdims=False)
    sent_part = lax.dynamic_index_in_dim(split, 1 - row_parity, 0, keepdims=False)
    sent_part, early_rows = lax.optimization_barrier((sent_part, grad_rows))
    back_third = lax.dot_general(
        early_rows, third_weight, (((1,), (1,)), ((), ())), preferred_element_type=jnp.float32
    )
    inner_grad = jnp.where(third_rows > 0, back_third, 0.0).astype(jnp.bfloat16)
    bits = devices.bit_length() - 1
    unit = channels // devices
    inner_tile = inner_grad.reshape(tile_rows, tile_width, channels)
    top = from_behind(inner_tile[-1:], "space", 2)
    bottom = from_behind(inner_tile[:1], "space", -2)

    def edge(tile):
        return jnp.where(col_parity == 0, tile[:, -1], tile[:, 0])

    rims = partner(
        jnp.concatenate([edge(top), edge(inner_tile), edge(bottom)], 0), "space", 0
    ).astype(jnp.float32)
    left = jnp.where(col_parity == 1, rims, 0.0)
    right = jnp.where(col_parity == 0, rims, 0.0)
    second_tile = to_tiles(kept_part, sent_part, col_parity, row_parity, row_bit)
    first_rows, local_term = group_backward(
        inner_grad,
        top[0],
        bottom[0],
        left,
        right,
        second_tile,
        group_weight,
        tile_rows,
        normalizer,
    )

    low_first = list(range(1, bits))
    high_first = [2, 1] + list(range(3, bits))
    third = []
    third_left = []
    for at in (0, 1):
        piece = halve_start(wgrad_half(third_rows, grad_rows, at, unit, normalizer), bits)
        third.append(piece)
        third_left.append(list(range(1, bits))[::-1])
    first_terms = [wgrad_half(input_rows, first_rows, at, unit, normalizer) for at in (0, 1)]
    group_pair = split_term(local_term, unit)
    third[0], third[1], _ = lax.optimization_barrier((third[0], third[1], first_rows))
    last = [halve_start(pair, bits) for pair in first_terms + [group_pair]]
    last_left = [list(range(1, bits))[::-1] for _ in last]
    last_order = [low_first, high_first, low_first]
    for at in range(len(high_first)):
        third = [
            halve_round(piece, left, order[at])
            for piece, left, order in zip(third, third_left, last_order)
        ]
        tied = lax.optimization_barrier((*third, *last))
        third, last = list(tied[:2]), list(tied[2:])
        last = [
            halve_round(piece, left, order[at])
            for piece, left, order in zip(last, last_left, last_order)
        ]
    third_wgrad = jnp.concatenate(third, -1)
    first_wgrad = jnp.concatenate(last[:2], -1)
    group_wgrad = last[2]
    first_rows, _ = lax.optimization_barrier((first_rows, first_terms[1][0]))
    summed = lax.dot_general(
        first_rows, first_weight, (((1,), (1,)), ((), ())), preferred_element_type=jnp.float32
    )
    input_grad = (
        (summed + grad_rows.astype(jnp.float32))
        .astype(jnp.bfloat16)
        .reshape(1, tile_rows, tile_width, channels)
    )
    return (input_grad, third_wgrad, group_wgrad, first_wgrad)


def solution(mesh):
    in_specs = (
        P(("parts", "space"), None, None, None),
        P(("parts", "space"), None, None, None),
        P(("parts", "space"), None, None, None),
        P(("parts", "space"), None, None, None),
        P(),
        P(),
        P(),
    )
    out_specs = (
        P(("parts", "space"), None, None, None),
        P(("parts", "space"), None),
        P(("parts", "space"), None),
        P(("parts", "space"), None),
    )
    return jax.shard_map(
        per_device, mesh=mesh, in_specs=in_specs, out_specs=out_specs, check_vma=False
    )
```

```python
import functools
import math

import jax
import jax.numpy as jnp
from jax import lax
from jax.experimental import pallas as pl
from jax.experimental.pallas import tpu as pltpu
from jax.sharding import PartitionSpec as P


def partner(block, axis, distance):
    count = lax.axis_size(axis)
    route = []
    for low in range(count):
        high = low | 1 << distance
        if high != low and high < count:
            route += [(low, high), (high, low)]
    return lax.ppermute(block, axis, route)


def from_behind(array, axis, by):
    count = lax.axis_size(axis)
    pairs = [(i, i + by) for i in range(count) if 0 <= i + by < count]
    return lax.ppermute(array, axis, pairs)


def halve_round(piece, left, bit):
    axis = left.index(bit)
    mine = lax.axis_index("space") // (1 << bit) % 2
    sent = lax.dynamic_index_in_dim(piece, 1 - mine, axis, keepdims=False)
    kept = lax.dynamic_index_in_dim(piece, mine, axis, keepdims=False)
    received = partner(sent.astype(jnp.bfloat16), "space", bit)
    left.remove(bit)
    return kept + received.astype(jnp.float32)


def halve_start(pair, bits):
    sent, kept = pair
    received = partner(shards_view(sent, bits - 1), "space", 0)
    return shards_view(kept, bits - 1) + received.astype(jnp.float32)


def shards_view(array, bits):
    rows, columns = array.shape
    return array.reshape((2,) * bits + (rows >> bits, columns))


def split_term(term, unit):
    mine = lax.axis_index("space") % 2
    view = term.reshape(-1, 2, unit, term.shape[1])
    sent = lax.dynamic_index_in_dim(view, 1 - mine, 1, keepdims=False)
    kept = lax.dynamic_index_in_dim(view, mine, 1, keepdims=False)
    columns = term.shape[1]
    return sent.astype(jnp.bfloat16).reshape(-1, columns), kept.reshape(-1, columns)


def wgrad_kernel(unit, normalizer, rows_ref, columns_ref, sent_ref, kept_ref):
    even = lax.axis_index("space") % 2 == 0
    term = lax.dot_general(
        rows_ref[...],
        columns_ref[...],
        (((0,), (0,)), ((), ())),
        preferred_element_type=jnp.float32,
    )
    term = term * normalizer
    sent, kept = [], []
    for at in range(0, term.shape[0], 2 * unit):
        low = term[at : at + unit]
        high = term[at + unit : at + 2 * unit]
        kept.append(jnp.where(even, low, high))
        sent.append(jnp.where(even, high, low))
    kept_ref[...] = jnp.concatenate(kept, 0)
    sent_ref[...] = jnp.concatenate(sent, 0).astype(jnp.bfloat16)


def wgrad_half(rows, columns, at, unit, normalizer):
    size, channels = rows.shape
    block = 256
    width = columns.shape[1] // 2
    out_spec = pl.BlockSpec((block // 2, width), lambda step: (step, 0))
    return pl.pallas_call(
        functools.partial(wgrad_kernel, unit, normalizer),
        grid=(channels // block,),
        in_specs=[
            pl.BlockSpec((size, block), lambda step: (0, step)),
            pl.BlockSpec((size, width), lambda step: (0, at)),
        ],
        out_specs=[out_spec, out_spec],
        out_shape=[
            jax.ShapeDtypeStruct((channels // 2, width), jnp.bfloat16),
            jax.ShapeDtypeStruct((channels // 2, width), jnp.float32),
        ],
        compiler_params=pltpu.CompilerParams(vmem_limit_bytes=24 * 2**20),
        cost_estimate=pl.CostEstimate(
            flops=2 * size * channels * width, bytes_accessed=6 * channels * width, transcendentals=0
        ),
    )(rows, columns)


def to_tiles(kept_part, sent_part, col_parity, row_parity, row_bit):
    tile_rows, double_cols, shard_width = kept_part.shape
    received = partner(sent_part, "space", row_bit)
    joined = jnp.where(
        row_parity == 0, jnp.stack([kept_part, received], 0), jnp.stack([received, kept_part], 0)
    )
    joined = joined.reshape(2, tile_rows, 2, double_cols // 2, shard_width)
    kept_cols = lax.dynamic_index_in_dim(joined, col_parity, 2, keepdims=False)
    sent_cols = lax.dynamic_index_in_dim(joined, 1 - col_parity, 2, keepdims=False)
    received_cols = partner(sent_cols, "space", 0)
    stacked = jnp.where(
        col_parity == 0,
        jnp.stack([kept_cols, received_cols], 1),
        jnp.stack([received_cols, kept_cols], 1),
    )
    return stacked.reshape(4, tile_rows * double_cols // 2, shard_width)


def group_kernel(
    tile_rows, width, group_width, normalizer,
    inner_ref, top_ref, bottom_ref, left_ref, right_ref, second_ref, weight_ref,
    first_ref, wgrad_ref, shifted, flipped,
):
    channels = inner_ref.shape[1]
    column = lax.broadcasted_iota(jnp.int32, (width, channels), 0)
    left = left_ref[...]
    right = right_ref[...]
    for y in range(tile_rows + 2):
        if y == 0:
            piece = top_ref[...]
        elif y == tile_rows + 1:
            piece = bottom_ref[...]
        else:
            piece = inner_ref[(y - 1) * width : y * width, :]
        wide = piece.astype(jnp.float32)
        before = jnp.where(column == width - 1, right[y : y + 1], pltpu.roll(wide, width - 1, 0))
        after = jnp.where(column == 0, left[y : y + 1], pltpu.roll(wide, 1, 0))
        for at, moved in enumerate((before, wide, after)):
            shifted[at, y * width : (y + 1) * width, :] = moved.astype(jnp.bfloat16)
            flipped[at, :, y * width : (y + 1) * width] = moved.T.astype(jnp.bfloat16)
    lanes = 128
    per = lanes // group_width
    own = (
        lax.broadcasted_iota(jnp.int32, (channels, channels), 0) // group_width
        == lax.broadcasted_iota(jnp.int32, (channels, channels), 1) // group_width
    )
    lane_group = lax.broadcasted_iota(jnp.int32, (channels, lanes), 1) // group_width

    def spread(array):
        step = group_width
        while step < lanes:
            array = array + pltpu.roll(array, step, 1)
            step *= 2
        return array

    second = second_ref[...]
    size = tile_rows * width
    back = jnp.zeros((size, channels), jnp.float32)
    row = None
    for tap in range(9):
        u, v = tap // 3 - 1, tap % 3 - 1
        start = (1 - u) * width
        chunk, slot = tap // per, tap % per
        if tap < 8:
            taps = weight_ref[:, chunk * lanes : (chunk + 1) * lanes].astype(jnp.float32)
            taps = jnp.where(lane_group == slot, taps, 0.0)
        else:
            taps = weight_ref[:, 8 * group_width : 9 * group_width].astype(jnp.float32)
            taps = jnp.concatenate(
                [taps, jnp.zeros((channels, lanes - group_width), jnp.float32)], 1
            )
        taps = spread(taps)
        dense = jnp.concatenate([taps] * (channels // lanes), 1)
        dense = jnp.where(own, dense, 0.0).astype(jnp.bfloat16)
        back = back + jnp.dot(
            shifted[v + 1, start : start + size, :], dense, preferred_element_type=jnp.float32
        )
        term = jnp.dot(
            flipped[v + 1, :, start : start + size], second, preferred_element_type=jnp.float32
        )
        term = jnp.where(own, term, 0.0)
        folded = term[:, :lanes]
        for at in range(1, channels // lanes):
            folded = folded + term[:, at * lanes : (at + 1) * lanes]
        folded = spread(folded) * normalizer
        row = folded if slot == 0 else jnp.where(lane_group == slot, folded, row)
        if slot == per - 1:
            wgrad_ref[:, chunk * lanes : (chunk + 1) * lanes] = row
        elif tap == 8:
            wgrad_ref[:, 8 * group_width : 9 * group_width] = row[:, :group_width]
    first_ref[...] = jnp.where(second > 0, back, 0.0).astype(jnp.bfloat16)


def group_backward(inner, top, bottom, left, right, second, weight, tile_rows, normalizer):
    size, channels = inner.shape
    width = size // tile_rows
    taps = weight.shape[1]
    block = second.shape[2]
    tall = tile_rows + 2

    def by_channels(rows):
        return pl.BlockSpec((rows, block), lambda at: (0, at))

    by_rows = pl.BlockSpec((block, taps), lambda at: (at, 0))
    return pl.pallas_call(
        functools.partial(group_kernel, tile_rows, width, taps // 9, normalizer),
        grid=(channels // block,),
        in_specs=[
            by_channels(size),
            by_channels(width),
            by_channels(width),
            by_channels(tall),
            by_channels(tall),
            pl.BlockSpec((None, size, block), lambda at: (at, 0, 0)),
            by_rows,
        ],
        out_specs=[by_channels(size), by_rows],
        out_shape=[
            jax.ShapeDtypeStruct((size, channels), jnp.bfloat16),
            jax.ShapeDtypeStruct((channels, taps), jnp.float32),
        ],
        scratch_shapes=[
            pltpu.VMEM((3, tall * width, block), jnp.bfloat16),
            pltpu.VMEM((3, block, tall * width), jnp.bfloat16),
        ],
        compiler_params=pltpu.CompilerParams(vmem_limit_bytes=32 * 2**20),
        cost_estimate=pl.CostEstimate(
            flops=90 * size * block * channels, bytes_accessed=8 * size * channels, transcendentals=0
        ),
    )(inner, top, bottom, left, right, second, weight)


def per_device(
    outer_grad, block_input, third_input, second_input, third_weight, group_weight, first_weight
):
    devices = lax.axis_size("space")
    position = lax.axis_index("space")
    row_bit = 1
    col_parity = position % 2
    row_parity = position // 2 % 2
    tile_rows = outer_grad.shape[1]
    tile_width = outer_grad.shape[2]
    channels = outer_grad.shape[3]
    normalizer = 1.0 / math.sqrt(tile_rows * tile_width * devices)
    grad_rows = outer_grad.reshape(tile_rows * tile_width, channels)
    third_rows = third_input.reshape(tile_rows * tile_width, channels)
    input_rows = block_input.reshape(tile_rows * tile_width, channels)
    split = second_input[0].reshape(2, tile_rows, 2 * tile_width, second_input.shape[3])
    kept_part = lax.dynamic_index_in_dim(split, row_parity, 0, keepdims=False)
    sent_part = lax.dynamic_index_in_dim(split, 1 - row_parity, 0, keepdims=False)
    sent_part, early_rows = lax.optimization_barrier((sent_part, grad_rows))
    back_third = lax.dot_general(
        early_rows, third_weight, (((1,), (1,)), ((), ())), preferred_element_type=jnp.float32
    )
    inner_grad = jnp.where(third_rows > 0, back_third, 0.0).astype(jnp.bfloat16)
    bits = devices.bit_length() - 1
    unit = channels // devices
    inner_tile = inner_grad.reshape(tile_rows, tile_width, channels)
    top = from_behind(inner_tile[-1:], "space", 2)
    bottom = from_behind(inner_tile[:1], "space", -2)

    def edge(tile):
        return jnp.where(col_parity == 0, tile[:, -1], tile[:, 0])

    rims = partner(
        jnp.concatenate([edge(top), edge(inner_tile), edge(bottom)], 0), "space", 0
    ).astype(jnp.float32)
    left = jnp.where(col_parity == 1, rims, 0.0)
    right = jnp.where(col_parity == 0, rims, 0.0)
    second_tile = to_tiles(kept_part, sent_part, col_parity, row_parity, row_bit)
    first_rows, local_term = group_backward(
        inner_grad,
        top[0],
        bottom[0],
        left,
        right,
        second_tile,
        group_weight,
        tile_rows,
        normalizer,
    )

    low_first = list(range(1, bits))
    high_first = [2, 1] + list(range(3, bits))
    third = []
    third_left = []
    for at in (0, 1):
        piece = halve_start(wgrad_half(third_rows, grad_rows, at, unit, normalizer), bits)
        third.append(piece)
        third_left.append(list(range(1, bits))[::-1])
    first_terms = [wgrad_half(input_rows, first_rows, at, unit, normalizer) for at in (0, 1)]
    group_pair = split_term(local_term, unit)
    third[0], third[1], _ = lax.optimization_barrier((third[0], third[1], first_rows))
    last = [halve_start(pair, bits) for pair in first_terms + [group_pair]]
    last_left = [list(range(1, bits))[::-1] for _ in last]
    last_order = [low_first, high_first, low_first]
    for at in range(len(high_first)):
        third = [
            halve_round(piece, left, order[at])
            for piece, left, order in zip(third, third_left, last_order)
        ]
        if at + 1 < len(high_first):
            tied = lax.optimization_barrier((*third, *last))
            third, last = list(tied[:2]), list(tied[2:])
        last = [
            halve_round(piece, left, order[at])
            for piece, left, order in zip(last, last_left, last_order)
        ]
    third_wgrad = jnp.concatenate(third, -1)
    first_wgrad = jnp.concatenate(last[:2], -1)
    group_wgrad = last[2]
    first_rows, _ = lax.optimization_barrier((first_rows, first_terms[1][0]))
    summed = lax.dot_general(
        first_rows, first_weight, (((1,), (1,)), ((), ())), preferred_element_type=jnp.float32
    )
    input_grad = (
        (summed + grad_rows.astype(jnp.float32))
        .astype(jnp.bfloat16)
        .reshape(1, tile_rows, tile_width, channels)
    )
    return (input_grad, third_wgrad, group_wgrad, first_wgrad)


def solution(mesh):
    in_specs = (
        P(("parts", "space"), None, None, None),
        P(("parts", "space"), None, None, None),
        P(("parts", "space"), None, None, None),
        P(("parts", "space"), None, None, None),
        P(),
        P(),
        P(),
    )
    out_specs = (
        P(("parts", "space"), None, None, None),
        P(("parts", "space"), None),
        P(("parts", "space"), None),
        P(("parts", "space"), None),
    )
    return jax.shard_map(
        per_device, mesh=mesh, in_specs=in_specs, out_specs=out_specs, check_vma=False
    )
```

```python
import functools
import math

import jax
import jax.numpy as jnp
from jax import lax
from jax.experimental import pallas as pl
from jax.experimental.pallas import tpu as pltpu
from jax.sharding import PartitionSpec as P


def partner(block, axis, distance):
    count = lax.axis_size(axis)
    route = []
    for low in range(count):
        high = low | 1 << distance
        if high != low and high < count:
            route += [(low, high), (high, low)]
    return lax.ppermute(block, axis, route)


def from_behind(array, axis, by):
    count = lax.axis_size(axis)
    pairs = [(i, i + by) for i in range(count) if 0 <= i + by < count]
    return lax.ppermute(array, axis, pairs)


def halve_round(piece, left, bit):
    axis = left.index(bit)
    mine = lax.axis_index("space") // (1 << bit) % 2
    sent = lax.dynamic_index_in_dim(piece, 1 - mine, axis, keepdims=False)
    kept = lax.dynamic_index_in_dim(piece, mine, axis, keepdims=False)
    received = partner(sent.astype(jnp.bfloat16), "space", bit)
    left.remove(bit)
    return kept + received.astype(jnp.float32)


def halve_start(pair, bits):
    sent, kept = pair
    received = partner(shards_view(sent, bits - 1), "space", 0)
    return shards_view(kept, bits - 1) + received.astype(jnp.float32)


def shards_view(array, bits):
    rows, columns = array.shape
    return array.reshape((2,) * bits + (rows >> bits, columns))


def split_term(term, unit):
    mine = lax.axis_index("space") % 2
    view = term.reshape(-1, 2, unit, term.shape[1])
    sent = lax.dynamic_index_in_dim(view, 1 - mine, 1, keepdims=False)
    kept = lax.dynamic_index_in_dim(view, mine, 1, keepdims=False)
    columns = term.shape[1]
    return sent.astype(jnp.bfloat16).reshape(-1, columns), kept.reshape(-1, columns)


def wgrad_kernel(unit, normalizer, rows_ref, columns_ref, sent_ref, kept_ref):
    even = lax.axis_index("space") % 2 == 0
    term = lax.dot_general(
        rows_ref[...],
        columns_ref[...],
        (((0,), (0,)), ((), ())),
        preferred_element_type=jnp.float32,
    )
    term = term * normalizer
    sent, kept = [], []
    for at in range(0, term.shape[0], 2 * unit):
        low = term[at : at + unit]
        high = term[at + unit : at + 2 * unit]
        kept.append(jnp.where(even, low, high))
        sent.append(jnp.where(even, high, low))
    kept_ref[...] = jnp.concatenate(kept, 0)
    sent_ref[...] = jnp.concatenate(sent, 0).astype(jnp.bfloat16)


def wgrad_half(rows, columns, at, unit, normalizer):
    size, channels = rows.shape
    block = 256
    width = columns.shape[1] // 2
    out_spec = pl.BlockSpec((block // 2, width), lambda step: (step, 0))
    return pl.pallas_call(
        functools.partial(wgrad_kernel, unit, normalizer),
        grid=(channels // block,),
        in_specs=[
            pl.BlockSpec((size, block), lambda step: (0, step)),
            pl.BlockSpec((size, width), lambda step: (0, at)),
        ],
        out_specs=[out_spec, out_spec],
        out_shape=[
            jax.ShapeDtypeStruct((channels // 2, width), jnp.bfloat16),
            jax.ShapeDtypeStruct((channels // 2, width), jnp.float32),
        ],
        compiler_params=pltpu.CompilerParams(vmem_limit_bytes=24 * 2**20),
        cost_estimate=pl.CostEstimate(
            flops=2 * size * channels * width, bytes_accessed=6 * channels * width, transcendentals=0
        ),
    )(rows, columns)


def to_tiles(kept_part, sent_part, col_parity, row_parity, row_bit):
    tile_rows, double_cols, shard_width = kept_part.shape
    received = partner(sent_part, "space", row_bit)
    joined = jnp.where(
        row_parity == 0, jnp.stack([kept_part, received], 0), jnp.stack([received, kept_part], 0)
    )
    joined = joined.reshape(2, tile_rows, 2, double_cols // 2, shard_width)
    kept_cols = lax.dynamic_index_in_dim(joined, col_parity, 2, keepdims=False)
    sent_cols = lax.dynamic_index_in_dim(joined, 1 - col_parity, 2, keepdims=False)
    received_cols = partner(sent_cols, "space", 0)
    stacked = jnp.where(
        col_parity == 0,
        jnp.stack([kept_cols, received_cols], 1),
        jnp.stack([received_cols, kept_cols], 1),
    )
    return stacked.reshape(4, tile_rows * double_cols // 2, shard_width)


def group_kernel(
    tile_rows, width, group_width, normalizer,
    inner_ref, top_ref, bottom_ref, left_ref, right_ref, second_ref, weight_ref,
    first_ref, wgrad_ref, shifted, flipped,
):
    channels = inner_ref.shape[1]
    column = lax.broadcasted_iota(jnp.int32, (width, channels), 0)
    left = left_ref[...]
    right = right_ref[...]
    for y in range(tile_rows + 2):
        if y == 0:
            piece = top_ref[...]
        elif y == tile_rows + 1:
            piece = bottom_ref[...]
        else:
            piece = inner_ref[(y - 1) * width : y * width, :]
        wide = piece.astype(jnp.float32)
        before = jnp.where(column == width - 1, right[y : y + 1], pltpu.roll(wide, width - 1, 0))
        after = jnp.where(column == 0, left[y : y + 1], pltpu.roll(wide, 1, 0))
        for at, moved in enumerate((before, wide, after)):
            shifted[at, y * width : (y + 1) * width, :] = moved.astype(jnp.bfloat16)
            flipped[at, :, y * width : (y + 1) * width] = moved.T.astype(jnp.bfloat16)
    lanes = 128
    per = lanes // group_width
    own = (
        lax.broadcasted_iota(jnp.int32, (channels, channels), 0) // group_width
        == lax.broadcasted_iota(jnp.int32, (channels, channels), 1) // group_width
    )
    lane_group = lax.broadcasted_iota(jnp.int32, (channels, lanes), 1) // group_width

    def spread(array):
        step = group_width
        while step < lanes:
            array = array + pltpu.roll(array, step, 1)
            step *= 2
        return array

    second = second_ref[...]
    size = tile_rows * width
    back = jnp.zeros((size, channels), jnp.float32)
    row = None
    for tap in range(9):
        u, v = tap // 3 - 1, tap % 3 - 1
        start = (1 - u) * width
        chunk, slot = tap // per, tap % per
        if tap < 8:
            taps = weight_ref[:, chunk * lanes : (chunk + 1) * lanes].astype(jnp.float32)
            taps = jnp.where(lane_group == slot, taps, 0.0)
        else:
            taps = weight_ref[:, 8 * group_width : 9 * group_width].astype(jnp.float32)
            taps = jnp.concatenate(
                [taps, jnp.zeros((channels, lanes - group_width), jnp.float32)], 1
            )
        taps = spread(taps)
        dense = jnp.concatenate([taps] * (channels // lanes), 1)
        dense = jnp.where(own, dense, 0.0).astype(jnp.bfloat16)
        back = back + jnp.dot(
            shifted[v + 1, start : start + size, :], dense, preferred_element_type=jnp.float32
        )
        term = jnp.dot(
            flipped[v + 1, :, start : start + size], second, preferred_element_type=jnp.float32
        )
        term = jnp.where(own, term, 0.0)
        folded = term[:, :lanes]
        for at in range(1, channels // lanes):
            folded = folded + term[:, at * lanes : (at + 1) * lanes]
        folded = spread(folded) * normalizer
        row = folded if slot == 0 else jnp.where(lane_group == slot, folded, row)
        if slot == per - 1:
            wgrad_ref[:, chunk * lanes : (chunk + 1) * lanes] = row
        elif tap == 8:
            wgrad_ref[:, 8 * group_width : 9 * group_width] = row[:, :group_width]
    first_ref[...] = jnp.where(second > 0, back, 0.0).astype(jnp.bfloat16)


def group_backward(inner, top, bottom, left, right, second, weight, tile_rows, normalizer):
    size, channels = inner.shape
    width = size // tile_rows
    taps = weight.shape[1]
    block = second.shape[2]
    tall = tile_rows + 2

    def by_channels(rows):
        return pl.BlockSpec((rows, block), lambda at: (0, at))

    by_rows = pl.BlockSpec((block, taps), lambda at: (at, 0))
    return pl.pallas_call(
        functools.partial(group_kernel, tile_rows, width, taps // 9, normalizer),
        grid=(channels // block,),
        in_specs=[
            by_channels(size),
            by_channels(width),
            by_channels(width),
            by_channels(tall),
            by_channels(tall),
            pl.BlockSpec((None, size, block), lambda at: (at, 0, 0)),
            by_rows,
        ],
        out_specs=[by_channels(size), by_rows],
        out_shape=[
            jax.ShapeDtypeStruct((size, channels), jnp.bfloat16),
            jax.ShapeDtypeStruct((channels, taps), jnp.float32),
        ],
        scratch_shapes=[
            pltpu.VMEM((3, tall * width, block), jnp.bfloat16),
            pltpu.VMEM((3, block, tall * width), jnp.bfloat16),
        ],
        compiler_params=pltpu.CompilerParams(vmem_limit_bytes=32 * 2**20),
        cost_estimate=pl.CostEstimate(
            flops=90 * size * block * channels, bytes_accessed=8 * size * channels, transcendentals=0
        ),
    )(inner, top, bottom, left, right, second, weight)


def per_device(
    outer_grad, block_input, third_input, second_input, third_weight, group_weight, first_weight
):
    devices = lax.axis_size("space")
    position = lax.axis_index("space")
    row_bit = 1
    col_parity = position % 2
    row_parity = position // 2 % 2
    tile_rows = outer_grad.shape[1]
    tile_width = outer_grad.shape[2]
    channels = outer_grad.shape[3]
    normalizer = 1.0 / math.sqrt(tile_rows * tile_width * devices)
    grad_rows = outer_grad.reshape(tile_rows * tile_width, channels)
    third_rows = third_input.reshape(tile_rows * tile_width, channels)
    input_rows = block_input.reshape(tile_rows * tile_width, channels)
    split = second_input[0].reshape(2, tile_rows, 2 * tile_width, second_input.shape[3])
    kept_part = lax.dynamic_index_in_dim(split, row_parity, 0, keepdims=False)
    sent_part = lax.dynamic_index_in_dim(split, 1 - row_parity, 0, keepdims=False)
    sent_part, early_rows = lax.optimization_barrier((sent_part, grad_rows))
    back_third = lax.dot_general(
        early_rows, third_weight, (((1,), (1,)), ((), ())), preferred_element_type=jnp.float32
    )
    inner_grad = jnp.where(third_rows > 0, back_third, 0.0).astype(jnp.bfloat16)
    bits = devices.bit_length() - 1
    unit = channels // devices
    inner_tile = inner_grad.reshape(tile_rows, tile_width, channels)
    top = from_behind(inner_tile[-1:], "space", 2)
    bottom = from_behind(inner_tile[:1], "space", -2)

    third_terms = [wgrad_half(third_rows, grad_rows, at, unit, normalizer) for at in (0, 1)]
    top, bottom, _ = lax.optimization_barrier((top, bottom, third_terms[1][0]))

    def edge(tile):
        return jnp.where(col_parity == 0, tile[:, -1], tile[:, 0])

    rims = partner(
        jnp.concatenate([edge(top), edge(inner_tile), edge(bottom)], 0), "space", 0
    ).astype(jnp.float32)
    left = jnp.where(col_parity == 1, rims, 0.0)
    right = jnp.where(col_parity == 0, rims, 0.0)
    second_tile = to_tiles(kept_part, sent_part, col_parity, row_parity, row_bit)
    first_rows, local_term = group_backward(
        inner_grad,
        top[0],
        bottom[0],
        left,
        right,
        second_tile,
        group_weight,
        tile_rows,
        normalizer,
    )

    low_first = list(range(1, bits))
    high_first = [2, 1] + list(range(3, bits))
    third = []
    third_left = []
    for at in (0, 1):
        piece = halve_start(third_terms[at], bits)
        third.append(piece)
        third_left.append(list(range(1, bits))[::-1])
    first_terms = [wgrad_half(input_rows, first_rows, at, unit, normalizer) for at in (0, 1)]
    group_pair = split_term(local_term, unit)
    third[0], third[1], _ = lax.optimization_barrier((third[0], third[1], first_rows))
    last = [halve_start(pair, bits) for pair in first_terms + [group_pair]]
    last_left = [list(range(1, bits))[::-1] for _ in last]
    last_order = [low_first, high_first, low_first]
    for at in range(len(high_first)):
        third = [
            halve_round(piece, left, order[at])
            for piece, left, order in zip(third, third_left, last_order)
        ]
        tied = lax.optimization_barrier((*third, *last))
        third, last = list(tied[:2]), list(tied[2:])
        last = [
            halve_round(piece, left, order[at])
            for piece, left, order in zip(last, last_left, last_order)
        ]
    third_wgrad = jnp.concatenate(third, -1)
    first_wgrad = jnp.concatenate(last[:2], -1)
    group_wgrad = last[2]
    first_rows, _ = lax.optimization_barrier((first_rows, first_terms[1][0]))
    summed = lax.dot_general(
        first_rows, first_weight, (((1,), (1,)), ((), ())), preferred_element_type=jnp.float32
    )
    input_grad = (
        (summed + grad_rows.astype(jnp.float32))
        .astype(jnp.bfloat16)
        .reshape(1, tile_rows, tile_width, channels)
    )
    return (input_grad, third_wgrad, group_wgrad, first_wgrad)


def solution(mesh):
    in_specs = (
        P(("parts", "space"), None, None, None),
        P(("parts", "space"), None, None, None),
        P(("parts", "space"), None, None, None),
        P(("parts", "space"), None, None, None),
        P(),
        P(),
        P(),
    )
    out_specs = (
        P(("parts", "space"), None, None, None),
        P(("parts", "space"), None),
        P(("parts", "space"), None),
        P(("parts", "space"), None),
    )
    return jax.shard_map(
        per_device, mesh=mesh, in_specs=in_specs, out_specs=out_specs, check_vma=False
    )
```
